32 devices in a mesh: section: 8 (over y, x, core), seq: 4 (over z).
Axes of the slice: x: 2, y: 2, z: 4, core: 2. Of those that a mesh axis runs over, the one named last changes fastest.
Arguments:
- grad_out: bfloat16 [8, 512, 2048], P('section', 'seq'), may hold values from -6 to 6
- block_input: bfloat16 [8, 512, 2048], P('section', 'seq'), may hold values from -5 to 5
- skip_saved: bfloat16 [8, 512, 2048], P('section', 'seq'), may hold values from -2 to 2
- saved_qkv: bfloat16 [8, 3, 512, 2048], P('section', None, None, 'seq'), may hold values from -16 to 16
- out_weight: bfloat16 [8, 2048, 2048], P('section', 'seq'), may hold values from -0.125 to 0.125
- qkv_weight: bfloat16 [8, 3, 2048, 2048], P('section', None, 'seq'), may hold values from -0.125 to 0.125
- gate: float32 [8, 2048], P('section'), may hold values from 0.5 to 1.5
- norm_scale: float32 [8, 2048], P('section'), may hold values from -0.5 to 0.5
- skip_gain: float32 [8, 2048], P('section'), may hold values from 0.3 to 1.5
Outputs:
- next_grad: bfloat16 [8, 512, 2048], P('section', 'seq')
- down_grad: bfloat16 [8, 512, 2048], P('section', 'seq')
- gain_grad: float32 [8, 2048], P('section')
The draws below stay inside these ranges and needn't reach their ends.
All inputs are finite; a program needn't handle non-finite values.
Results may differ from the reference program's by a relative error of at most 0.015.
Values may be sent and summed in bfloat16 or wider, within the bound.
No kernel may reach another device: no remote copies, remote signals or barrier semaphores. Data moves between devices by JAX's collectives and lax.ppermute only.
A program may use at most 128 MiB of HBM per device.

```python
import math
import jax
import jax.numpy as jnp
from jax import lax

D = 2048
HEADS = 16
HEAD_DIM = 128
TOKENS = 512
SECTIONS = 8
N_SEQ = 4


def draw_saved_qkv(key, part):
    width = HEADS * HEAD_DIM
    key_base = jax.random.fold_in(key, 0)
    values = jnp.clip(jax.random.normal(key_base, (SECTIONS, 3, TOKENS, width), jnp.float32), -4.0, 4.0)
    return values.astype(jnp.bfloat16)


def draw_block_input(key, part):
    key_base, key_rows, key_cols = jax.random.split(key, 3)
    row_scale = jnp.exp(jax.random.uniform(key_rows, (SECTIONS, TOKENS, 1), jnp.float32, math.log(0.01), math.log(0.1)))
    col_scale = jnp.exp(jax.random.uniform(key_cols, (SECTIONS, 1, D), jnp.float32, 0.0, math.log(10.0)))
    base = jnp.clip(jax.random.normal(key_base, (SECTIONS, TOKENS, D), jnp.float32), -4.0, 4.0)
    return (base * row_scale * col_scale).astype(jnp.bfloat16)


def draw_skip_saved(key, part):
    position = jnp.arange(TOKENS).astype(jnp.float32)[None, :, None]
    rising = (1.0 + 2.0 * position / (TOKENS - 1)) * TOKENS ** (-0.5)
    base = jnp.clip(jax.random.normal(key, (SECTIONS, TOKENS, D), jnp.float32), -4.0, 4.0)
    return jnp.clip(base * rising, -2.0, 2.0).astype(jnp.bfloat16)


def steps_of(rng, dims, cuts, least, largest):
    def one(dim, parts):
        steps = jax.random.uniform(jax.random.fold_in(jax.random.fold_in(rng, 6), dim), (parts,), jnp.float32, least / len(cuts), largest / len(cuts))
        return jnp.repeat(jnp.exp(steps), dims[dim] // parts).reshape((-1,) + (1,) * (len(dims) - dim - 1))

    loudness = one(*cuts[0])
    for cut in cuts[1:]:
        loudness = loudness * one(*cut)
    return loudness


def normal_values(rng, extent, spread, bound, shards=(), dtype=jnp.bfloat16):
    drawn = jax.random.normal(rng, extent, jnp.float32) * spread
    if len(shards) > 0:
        drawn = steps_of(rng, extent, shards, -0.22, 0.18) * drawn
    return jnp.clip(drawn, min=-bound, max=bound).astype(dtype)


def setup_inputs(seed: int = 0) -> dict:
    streams_of = jax.random.split(jax.random.key(seed), 10)
    return {
        "grad_out": normal_values(streams_of[0], (SECTIONS, TOKENS, D), 1.0, 6.0, ((0, 8), (1, 4))),
        "block_input": draw_block_input(jax.random.fold_in(streams_of[9], 71), 0),
        "skip_saved": draw_skip_saved(jax.random.fold_in(streams_of[9], 71), 0),
        "saved_qkv": draw_saved_qkv(jax.random.fold_in(streams_of[9], 71), 0),
        "out_weight": normal_values(streams_of[4], (SECTIONS, HEADS * HEAD_DIM, D), (HEADS * HEAD_DIM) ** -0.5, 0.125, ((0, 8), (1, 4))),
        "qkv_weight": normal_values(streams_of[5], (SECTIONS, 3, HEADS * HEAD_DIM, D), D ** -0.5, 0.125, ((0, 8), (2, 4))),
        "gate": jnp.clip(0.5 + 1.0 * jax.random.uniform(streams_of[6], (SECTIONS, D), jnp.float32) ** steps_of(streams_of[6], (SECTIONS, D), ((0, 8),), -0.2, 0.2), 0.5, 1.5),
        "norm_scale": jnp.clip(jax.random.uniform(streams_of[7], (SECTIONS, D), jnp.float32, -0.5, 0.5) * steps_of(streams_of[7], (SECTIONS, D), ((0, 8),), -0.4, 0.0), -0.5, 0.5),
        "skip_gain": jnp.clip(0.3 + 1.2 * jax.random.uniform(streams_of[8], (SECTIONS, D), jnp.float32) ** steps_of(streams_of[8], (SECTIONS, D), ((0, 8),), -0.2, 0.2), 0.3, 1.5),
    }


def head_backward(inputs):
    query, keys, values, grad_head = inputs
    factor = HEAD_DIM ** (-0.5)
    scores = jnp.dot(query, keys.T, preferred_element_type=jnp.float32) * factor
    scores = scores - lax.optimization_barrier(jnp.max(scores, axis=-1, keepdims=True))
    weights = jnp.exp(scores)
    probs = weights / lax.optimization_barrier(jnp.sum(weights, axis=-1, keepdims=True))
    dprobs = jnp.dot(grad_head, values.T, preferred_element_type=jnp.float32)
    delta = lax.optimization_barrier(jnp.sum(probs * dprobs, axis=-1, keepdims=True))
    dscores = probs * (dprobs - delta)
    probs_low = probs.astype(jnp.bfloat16)
    dscores_low = dscores.astype(jnp.bfloat16)
    grad_query = (jnp.dot(dscores_low, keys, preferred_element_type=jnp.float32) * factor).astype(jnp.bfloat16)
    grad_keys = (jnp.dot(dscores_low.T, query, preferred_element_type=jnp.float32) * factor).astype(jnp.bfloat16)
    grad_values = jnp.dot(probs_low.T, grad_head, preferred_element_type=jnp.float32).astype(jnp.bfloat16)
    return (grad_query, grad_keys, grad_values)

def add_feature(total, paired_values):
    partial_term = jnp.dot(paired_values[0], paired_values[1].T, preferred_element_type=jnp.float32)
    rounded = lax.optimization_barrier(partial_term.astype(jnp.bfloat16))
    return (total + rounded.astype(jnp.float32), None)

def add_heads(total, paired_values):
    partial_term = jnp.einsum('wqg,wgj->qj', paired_values[0].astype(jnp.float32), paired_values[1].astype(jnp.float32))
    rounded = lax.optimization_barrier(partial_term.astype(jnp.bfloat16))
    return (total + rounded.astype(jnp.float32), None)

def section_backward(inputs):
    incoming_gradient, block_in, skip_in, qkv_in, weight_out, weight_qkv, gate_row, scale_row, gain_row, last_flag = inputs
    width = HEADS * HEAD_DIM
    feat_group = D // N_SEQ
    head_group = HEADS // N_SEQ
    gated = (incoming_gradient.astype(jnp.float32) * gate_row).astype(jnp.bfloat16)
    gated_groups = jnp.moveaxis(gated.reshape(TOKENS, N_SEQ, feat_group), 1, 0)
    weight_groups = jnp.moveaxis(weight_out.reshape(width, N_SEQ, feat_group), 1, 0)
    summed, _ = lax.scan(add_feature, jnp.zeros((TOKENS, width), jnp.float32), (gated_groups, weight_groups))
    attn_grad = summed.astype(jnp.bfloat16)

    def by_heads(matrix):
        return jnp.moveaxis(matrix.reshape(TOKENS, HEADS, HEAD_DIM), 1, 0)
    grad_query, grad_keys, grad_values = lax.map(head_backward, (by_heads(qkv_in[0]), by_heads(qkv_in[1]), by_heads(qkv_in[2]), by_heads(attn_grad)))
    stacked = jnp.stack([grad_query, grad_keys, grad_values], 0)
    stacked = stacked.reshape(3, N_SEQ, head_group, TOKENS, HEAD_DIM)
    stacked = jnp.transpose(stacked, (1, 0, 3, 2, 4)).reshape(N_SEQ, 3, TOKENS, head_group * HEAD_DIM)
    weight_parts = jnp.moveaxis(weight_qkv.reshape(3, N_SEQ, head_group * HEAD_DIM, D), 1, 0)
    normed_grad, _ = lax.scan(add_heads, jnp.zeros((TOKENS, D), jnp.float32), (stacked, weight_parts))
    xval = block_in.astype(jnp.float32)
    mean_x = lax.optimization_barrier(jnp.mean(xval, axis=-1, keepdims=True))
    centered_input = xval - mean_x
    var_x = lax.optimization_barrier(jnp.mean(centered_input * centered_input, axis=-1, keepdims=True))
    inverse_deviation = 1.0 / jnp.sqrt(var_x + 1e-06)
    normalized_input = centered_input * inverse_deviation
    scaled_gradient = normed_grad * (1.0 + scale_row)
    input_gradient = incoming_gradient.astype(jnp.float32) + inverse_deviation * (scaled_gradient - lax.optimization_barrier(jnp.mean(scaled_gradient, axis=-1, keepdims=True)) - normalized_input * lax.optimization_barrier(jnp.mean(scaled_gradient * normalized_input, axis=-1, keepdims=True)))
    hand_grad = input_gradient.astype(jnp.bfloat16)
    mirror_grad = ((gain_row + last_flag) * input_gradient).astype(jnp.bfloat16)
    gain_grad = lax.optimization_barrier(jnp.sum(input_gradient * skip_in.astype(jnp.float32), axis=0))
    return (hand_grad, mirror_grad, gain_grad)

def reference(grad_out, block_input, skip_saved, saved_qkv, out_weight, qkv_weight, gate, norm_scale, skip_gain):
    last_flags = (jnp.arange(SECTIONS) == SECTIONS - 1).astype(jnp.float32)[:, None]
    hand_grad, down_grad, gain_grad = lax.map(section_backward, (grad_out, block_input, skip_saved, saved_qkv, out_weight, qkv_weight, gate, norm_scale, skip_gain, last_flags))
    next_grad = jnp.concatenate([jnp.zeros((1, TOKENS, D), jnp.bfloat16), hand_grad[:-1]], axis=0)
    return (next_grad, down_grad, gain_grad)
```

```python
import functools

import jax
import jax.numpy as jnp
from jax import lax
from jax.experimental import pallas as pl
from jax.experimental.pallas import tpu as pltpu
from jax.sharding import PartitionSpec as P

HEAD_DIM = 128

norm_eps = 1e-06


NT = (((1,), (1,)), ((), ()))
NN = (((1,), (0,)), ((), ()))
TN = (((0,), (0,)), ((), ()))


def mm(a, b, dims):
    return lax.dot_general(a, b, dims, preferred_element_type=jnp.float32)


def passed_along(block, axis, distance):
    devices = range(lax.axis_size(axis))
    route = [(i - distance, i) for i in devices if i - distance in devices]
    return lax.ppermute(block, axis, route)


VMEM_SPEC = pl.BlockSpec(memory_space=pltpu.VMEM)
SMEM_SPEC = pl.BlockSpec(memory_space=pltpu.SMEM)


def attend(slots, seq_index, block_refs, gate_ref, weight_ref, qkv_ref, gated_ref, query_ref, dq_ref, visit):
    rows = block_refs[0].shape[0]
    width = weight_ref.shape[0]
    factor = HEAD_DIM ** (-0.5)
    for place, slot in enumerate(slots):
        start = pl.multiple_of((seq_index ^ slot) * rows, rows)
        here = pl.ds(place * rows, rows)
        gated_ref[here, :] = (block_refs[place][...].astype(jnp.float32) * gate_ref[...]).astype(jnp.bfloat16)
        query_ref[here, :] = qkv_ref[0, pl.ds(start, rows), :]
    attn = mm(gated_ref[...], weight_ref[...], NT).astype(jnp.bfloat16)
    for head in range(width // HEAD_DIM):
        cols = slice(head * HEAD_DIM, (head + 1) * HEAD_DIM)
        query = query_ref[:, cols]
        keys = qkv_ref[1, :, cols]
        values = qkv_ref[2, :, cols]
        grad = attn[:, cols]
        scores = mm(keys, query, NT) * factor
        weights = jnp.exp(scores - jnp.max(scores, axis=0, keepdims=True))
        probs = weights / jnp.sum(weights, axis=0, keepdims=True)
        dprobs = mm(values, grad, NT)
        delta = jnp.sum(probs * dprobs, axis=0, keepdims=True)
        dscores = (probs * (dprobs - delta)).astype(jnp.bfloat16)
        dq = mm(keys, dscores, TN) * factor
        dq_ref[:, cols] = dq.T.astype(jnp.bfloat16)
        visit(cols, mm(dscores, query, NN), mm(probs.astype(jnp.bfloat16), grad, NN))


def first_kernel(index_ref, own_ref, one_ref, two_ref, gate_ref, weight_ref, qkv_ref, dq_ref, dk_ref, dv_ref, gated_ref, query_ref):
    def visit(cols, dk, dv):
        dk_ref[:, cols] = dk
        dv_ref[:, cols] = dv

    attend((0, 1, 2), index_ref[0], (own_ref, one_ref, two_ref), gate_ref, weight_ref, qkv_ref, gated_ref, query_ref, dq_ref, visit)


def project(left_ref, weight_ref, store):
    width = weight_ref.shape[1]
    step = min(512, width)
    for low in range(0, width, step):
        cols = slice(low, low + step)
        store(cols, mm(left_ref[...], weight_ref[:, cols], NN))


def last_kernel(
    index_ref, far_a_ref, far_b_ref, gate_ref, weight_ref, qkv_ref, dk_in_ref, dv_in_ref, proj_ref,
    out_ref, dk_ref, dv_ref, far_ref, gated_ref, query_ref, left_ref,
):
    rows, width = query_ref.shape
    factor = HEAD_DIM ** (-0.5)
    index = index_ref[0]
    far_ref[...] = jnp.where((index == 1) | (index == 2), far_b_ref[...], far_a_ref[...])

    def visit(cols, dk, dv):
        dk_ref[:, cols] = ((dk_in_ref[:, cols] + dk) * factor).astype(jnp.bfloat16)
        dv_ref[:, cols] = (dv_in_ref[:, cols] + dv).astype(jnp.bfloat16)

    attend((3,), index, (far_ref,), gate_ref, weight_ref, qkv_ref, gated_ref, query_ref, left_ref.at[:, pl.ds(0, width)], visit)
    start = pl.multiple_of((index ^ 3) * rows, rows)
    left_ref[:, width : 2 * width] = dk_ref[pl.ds(start, rows), :]
    left_ref[:, 2 * width :] = dv_ref[pl.ds(start, rows), :]

    def store(cols, value):
        out_ref[:, cols] = value.astype(jnp.bfloat16)

    project(left_ref, proj_ref, store)


def rest_kernel(index_ref, dq_ref, dk_ref, dv_ref, proj_ref, own_ref, one_ref, two_ref, left_ref):
    total, width = dq_ref.shape
    rows = total // 3
    index = index_ref[0]
    left_ref[:, :width] = dq_ref[...]
    for slot in range(3):
        start = pl.multiple_of((index ^ slot) * rows, rows)
        here = pl.ds(slot * rows, rows)
        left_ref[here, width : 2 * width] = dk_ref[pl.ds(start, rows), :]
        left_ref[here, 2 * width :] = dv_ref[pl.ds(start, rows), :]

    def store(cols, value):
        own_ref[:, cols] = value[:rows]
        one_ref[:, cols] = value[rows : 2 * rows].astype(jnp.bfloat16)
        two_ref[:, cols] = value[2 * rows :]

    project(left_ref, proj_ref, store)


def norm_kernel(flag_ref, own_ref, one_ref, two_ref, mid_ref, grad_ref, input_ref, skip_ref, scale_ref, gain_ref, hand_ref, down_ref, sum_ref):
    rows, features = own_ref.shape
    step = 16
    sum_ref[...] = jnp.zeros_like(sum_ref)

    def visit(i, carry):
        here = pl.ds(pl.multiple_of(i * step, step), step)
        f32 = jnp.float32
        normed = own_ref[here, :] + one_ref[here, :].astype(f32) + two_ref[here, :].astype(f32) + mid_ref[here, :].astype(f32)
        scaled = normed * (1.0 + scale_ref[...])
        value = input_ref[here, :].astype(f32)
        centered = value - jnp.mean(value, axis=-1, keepdims=True)
        var = jnp.mean(centered * centered, axis=-1, keepdims=True)
        rstd = 1.0 / jnp.sqrt(var + norm_eps)
        xhat = centered * rstd
        result = grad_ref[here, :].astype(f32) + rstd * (
            scaled - jnp.mean(scaled, axis=-1, keepdims=True) - xhat * jnp.mean(scaled * xhat, axis=-1, keepdims=True)
        )
        hand_ref[here, :] = result.astype(jnp.bfloat16)
        down_ref[here, :] = ((gain_ref[...] + flag_ref[0]) * result).astype(jnp.bfloat16)
        sum_ref[...] += jnp.sum(result * skip_ref[here, :].astype(f32), axis=0, keepdims=True)
        return carry

    lax.fori_loop(0, rows // step, visit, 0)


def call(kernel, args, outs, scratch=(), flops=0, moved=0):
    return pl.pallas_call(
        kernel,
        out_shape=outs,
        in_specs=[SMEM_SPEC] + [VMEM_SPEC] * (len(args) - 1),
        out_specs=jax.tree.map(lambda _: VMEM_SPEC, outs),
        scratch_shapes=list(scratch),
        cost_estimate=pl.CostEstimate(flops=flops, bytes_accessed=moved, transcendentals=0),
    )(*args)


def four_on_device(grad_out, block_input, skip_saved, saved_qkv, out_weight, qkv_weight, gate, norm_scale, skip_gain):
    bf16, f32 = jnp.bfloat16, jnp.float32
    sds = jax.ShapeDtypeStruct
    incoming = grad_out[0]
    rows, features = incoming.shape
    width = out_weight.shape[1]
    tokens = 4 * rows
    index = lax.axis_index("seq").astype(jnp.int32).reshape(1)
    qkv = saved_qkv[0]
    weight_out = out_weight[0]
    weight_qkv = qkv_weight[0].reshape(3 * width, features)

    swap_one = [(i, i ^ 1) for i in range(4)]
    swap_two = [(i, i ^ 2) for i in range(4)]
    swap_mid = [(1, 2), (2, 1)]
    outward = [(1, 0), (2, 3)]
    inward = [(0, 1), (3, 2)]

    def moved(block, route):
        return lax.ppermute(block, "seq", route)

    two = moved(incoming, swap_two)
    one = moved(incoming, swap_one)
    far_a = moved(two, outward)
    far_b = moved(incoming, swap_mid)

    dq, dk_part, dv_part = call(
        first_kernel,
        (index, incoming, one, two, gate, weight_out, qkv),
        (sds((3 * rows, width), bf16), sds((tokens, width), f32), sds((tokens, width), f32)),
        (pltpu.VMEM((3 * rows, features), bf16), pltpu.VMEM((3 * rows, width), bf16)),
        flops=2 * 3 * rows * width * (features + 5 * tokens),
        moved=2 * (3 * rows * features + width * features + 3 * tokens * width) + 8 * tokens * width,
    )
    send_far, dk, dv = call(
        last_kernel,
        (index, far_a, far_b, gate, weight_out, qkv, dk_part, dv_part, weight_qkv),
        (sds((rows, features), bf16), sds((tokens, width), bf16), sds((tokens, width), bf16)),
        (
            pltpu.VMEM((rows, features), bf16), pltpu.VMEM((rows, features), bf16),
            pltpu.VMEM((rows, width), bf16), pltpu.VMEM((rows, 3 * width), bf16),
        ),
        flops=2 * rows * width * (4 * features + 5 * tokens),
        moved=2 * (3 * rows * features + 4 * width * features + 3 * tokens * width) + 8 * tokens * width,
    )
    from_end = moved(send_far, inward)
    from_mid = moved(send_far, swap_mid)
    part_own, send_one, part_two = call(
        rest_kernel,
        (index, dq, dk, dv, weight_qkv),
        (sds((rows, features), f32), sds((rows, features), bf16), sds((rows, features), f32)),
        (pltpu.VMEM((3 * rows, 3 * width), bf16),),
        flops=2 * 3 * rows * 3 * width * features,
        moved=2 * (3 * width * features + 9 * rows * width) + 10 * rows * features,
    )
    from_one = moved(send_one, swap_one)
    send_two = (part_two + from_end.astype(f32)).astype(bf16)
    from_two = moved(send_two, swap_two)

    last_flag = (lax.axis_index("section") == lax.axis_size("section") - 1).astype(f32).reshape(1)
    hand, down, gain_local = call(
        norm_kernel,
        (last_flag, part_own, from_one, from_two, from_mid, incoming, block_input[0], skip_saved[0], norm_scale, skip_gain),
        (sds((rows, features), bf16), sds((rows, features), bf16), sds((1, features), f32)),
        flops=40 * rows * features,
        moved=20 * rows * features,
    )
    next_grad = passed_along(hand, "section", 1)
    gain = gain_local
    for mask in (1, 2, 3):
        gain = gain + moved(gain_local, [(i, i ^ mask) for i in range(4)])
    return (next_grad[None], down[None], gain)


def local_attention(query_all, keys_all, values_all, grad_cols, head_count, head_size):
    factor = head_size ** (-0.5)
    total_rows = query_all.shape[0]
    block_rows = min(512, total_rows)
    block_count = total_rows // block_rows
    query_out, keys_out, values_out = ([], [], [])
    for head_idx in range(head_count):
        lower = head_idx * head_size
        query_head = query_all[:, lower : lower + head_size]
        keys_head = keys_all[:, lower : lower + head_size]
        values_head = values_all[:, lower : lower + head_size]
        grad_head = grad_cols[lower : lower + head_size, :]
        query_blocks = query_head.reshape(block_count, block_rows, head_size)
        grad_blocks = jnp.moveaxis(grad_head.reshape(head_size, block_count, block_rows), 1, 0)

        def visit(carried, blocks):
            keys_acc, values_acc = carried
            query_blk, grad_blk = blocks
            scores = (
                jnp.einsum("qd,kd->qk", query_blk, keys_head, preferred_element_type=jnp.float32)
                * factor
            )
            scores = scores - jnp.max(scores, axis=-1, keepdims=True)
            weights = jnp.exp(scores)
            probs = weights / jnp.sum(weights, axis=-1, keepdims=True)
            dprobs = jnp.einsum(
                "dq,kd->qk", grad_blk, values_head, preferred_element_type=jnp.float32
            )
            delta = jnp.sum(probs * dprobs, axis=-1, keepdims=True)
            dscores = probs * (dprobs - delta)
            probs_low = probs.astype(jnp.bfloat16)
            dscores_low = dscores.astype(jnp.bfloat16)
            values_acc = values_acc + jnp.einsum(
                "qk,dq->kd", probs_low, grad_blk, preferred_element_type=jnp.float32
            )
            keys_acc = keys_acc + jnp.einsum(
                "qk,qd->kd", dscores_low, query_blk, preferred_element_type=jnp.float32
            )
            query_grad = (
                jnp.einsum("qk,kd->qd", dscores_low, keys_head, preferred_element_type=jnp.float32)
                * factor
            ).astype(jnp.bfloat16)
            return ((keys_acc, values_acc), query_grad)

        empty = jnp.zeros((total_rows, head_size), jnp.float32)
        (keys_acc, values_acc), query_grads = lax.scan(
            visit, (empty, empty), (query_blocks, grad_blocks)
        )
        query_out.append(query_grads.reshape(total_rows, head_size))
        keys_out.append((keys_acc * factor).astype(jnp.bfloat16))
        values_out.append(values_acc.astype(jnp.bfloat16))
    return (
        jnp.concatenate(query_out, axis=1),
        jnp.concatenate(keys_out, axis=1),
        jnp.concatenate(values_out, axis=1),
    )


def any_on_device(
    grad_out,
    block_input,
    skip_saved,
    saved_qkv,
    out_weight,
    qkv_weight,
    gate,
    norm_scale,
    skip_gain,
):
    seq_count = lax.axis_size("seq")
    incoming_gradient = grad_out[0]
    tok_rows, features = incoming_gradient.shape
    local_width = out_weight.shape[1]
    head_size = HEAD_DIM
    head_count = local_width // head_size
    feat_group = features // seq_count
    gated = (incoming_gradient.astype(jnp.float32) * gate[0]).astype(jnp.bfloat16)
    weight_out = out_weight[0]
    rows_in = lax.all_gather(gated, "seq", axis=0, tiled=True)
    row_count = rows_in.shape[0]
    terms = jnp.einsum(
        "rgs,hgs->ghr",
        rows_in.reshape(row_count, seq_count, feat_group),
        weight_out.reshape(local_width, seq_count, feat_group),
        preferred_element_type=jnp.float32,
    )
    rounded = lax.optimization_barrier(terms.astype(jnp.bfloat16))
    grad_cols = jnp.sum(rounded.astype(jnp.float32), axis=0).astype(jnp.bfloat16)
    query_grad, keys_grad, values_grad = local_attention(
        saved_qkv[0, 0], saved_qkv[0, 1], saved_qkv[0, 2], grad_cols, head_count, head_size
    )
    weight_qkv = qkv_weight[0]
    total = jnp.dot(query_grad, weight_qkv[0], preferred_element_type=jnp.float32)
    total = total + jnp.dot(keys_grad, weight_qkv[1], preferred_element_type=jnp.float32)
    total = total + jnp.dot(values_grad, weight_qkv[2], preferred_element_type=jnp.float32)
    normed_grad = lax.psum_scatter(
        total.astype(jnp.bfloat16), "seq", scatter_dimension=0, tiled=True
    ).astype(jnp.float32)
    xvalue = block_input[0].astype(jnp.float32)
    mean_x = jnp.mean(xvalue, axis=-1, keepdims=True)
    centered_input = xvalue - mean_x
    var_x = jnp.mean(centered_input * centered_input, axis=-1, keepdims=True)
    inverse_deviation = 1.0 / jnp.sqrt(var_x + norm_eps)
    normalized_input = centered_input * inverse_deviation
    scaled_gradient = normed_grad * (1.0 + norm_scale[0])
    input_gradient = incoming_gradient.astype(jnp.float32) + inverse_deviation * (
        scaled_gradient
        - jnp.mean(scaled_gradient, axis=-1, keepdims=True)
        - normalized_input * jnp.mean(scaled_gradient * normalized_input, axis=-1, keepdims=True)
    )
    hand_grad = input_gradient.astype(jnp.bfloat16)
    next_grad = passed_along(hand_grad, "section", 1)
    last_flag = jnp.where(
        lax.axis_index("section") == lax.axis_size("section") - 1, 1.0, 0.0
    ).astype(jnp.float32)
    down_grad = ((skip_gain[0] + last_flag) * input_gradient).astype(jnp.bfloat16)
    gain_local = jnp.sum(input_gradient * skip_saved[0].astype(jnp.float32), axis=0)
    gain_grad = lax.psum(gain_local, "seq")
    return (next_grad[None], down_grad[None], gain_grad[None])


def solution(mesh):
    placed = (
        P("section", "seq", None),
        P("section", "seq", None),
        P("section", "seq", None),
        P("section", None, None, "seq"),
        P("section", "seq", None),
        P("section", None, "seq", None),
        P("section", None),
        P("section", None),
        P("section", None),
    )
    return jax.shard_map(
        four_on_device if mesh.shape["seq"] == 4 else any_on_device,
        mesh=mesh,
        in_specs=placed,
        out_specs=(P("section", "seq", None), P("section", "seq", None), P("section", None)),
        check_vma=False,
    )
```
